512 devices in a mesh: tp: 8 (over x, y_hi), seq: 64 (over z, y_lo, core).
Axes of the slice: x: 4, y: 8 (y_hi: 2, y_lo: 4; y = y_hi * 4 + y_lo), z: 8, core: 2. Of those that a mesh axis runs over, the one named last changes fastest.
Arguments:
- llama_context: bfloat16 [512, 4096], P(None, 'tp'), may hold values from -6 to 6
- llama_residual: bfloat16 [512, 4096], P(None, 'seq'), may hold values from -6 to 6
- w_attn_out: bfloat16 [4096, 4096], P('tp', 'seq'), may hold values from -0.09375 to 0.09375
- w_caption: bfloat16 [4096, 2560], P('seq', 'tp'), may hold values from -0.09375 to 0.09375
- w_text_kv: bfloat16 [2560, 2, 2048], P(None, None, 'tp'), may hold values from -0.125 to 0.125
- prompt_length: int32 [4], replicated, may hold values from 1 to 128, as said below
- image_query: bfloat16 [2, 16384, 2048], P(None, 'seq', 'tp'), may hold values from -32 to 32
- image_key: bfloat16 [2, 16384, 2048], P(None, 'seq', 'tp'), may hold values from -9 to 9
- image_value: bfloat16 [2, 16384, 2048], P(None, 'seq', 'tp'), may hold values from -6 to 6
Outputs:
- joint_context: bfloat16 [2, 16384, 2048], P(None, 'seq', 'tp')
The draws below stay inside these ranges and needn't reach their ends.
Inputs may be any that keep to these rules, and one draw needn't show every extreme that they name: `prompt_length`: one pair's prompt has all 128 tokens live, every other pair's fewer.
All inputs are finite; a program needn't handle non-finite values.
Results may differ from the reference program's by a relative error of at most 0.039.
Values may be sent and summed in bfloat16 or wider, within the bound.
No kernel may reach another device: no remote copies, remote signals or barrier semaphores. Data moves between devices by JAX's collectives and lax.ppermute only.
A program may use at most 64 MiB of HBM per device.

```python
import math
import jax
import jax.numpy as jnp
from jax import lax

DL = 4096
TXT = 128
D = 2560
HEADS = 16
HD = 128
IMG = 4096
PAIRS = 4
N_TP = 8


def draw_prompt_length(key, part):
    base = jax.random.fold_in(key, 777)
    pick_key, length_key = jax.random.split(base, 2)
    full_pair = jax.random.randint(pick_key, (), 0, PAIRS)
    shorter = jax.random.randint(length_key, (PAIRS,), 1, TXT)
    places = jnp.arange(PAIRS, dtype=jnp.int32)
    return jnp.where(places == full_pair, TXT, shorter).astype(jnp.int32)


def attention_pair(key):
    base = jax.random.fold_in(key, 4242)
    first_key, second_key = jax.random.split(base, 2)
    extent = (2, PAIRS * IMG, HEADS * HD)
    queries = jnp.clip(1.4 * jax.random.normal(first_key, extent, jnp.float32), -8.4, 8.4)
    key_rows = jnp.clip(1.4 * jax.random.normal(second_key, extent, jnp.float32), -8.4, 8.4)
    return (queries, key_rows)


def draw_image_query(key, part):
    return attention_pair(key)[0].astype(jnp.bfloat16)


def draw_image_key(key, part):
    return attention_pair(key)[1].astype(jnp.bfloat16)


def shard_levels(key, shape, pieces, low, largest):
    loudness = 1.0
    for dim, shards_of in pieces:
        draws = jax.random.uniform(jax.random.fold_in(jax.random.fold_in(key, 6), dim), (shards_of,), jnp.float32, low / len(pieces), largest / len(pieces))
        loudness = loudness * jnp.repeat(jnp.exp(draws), shape[dim] // shards_of).reshape((-1,) + (1,) * (len(shape) - 1 - dim))
    return loudness


def centred(own_key, dims, deviation, reach, cuts=(), kind=jnp.bfloat16):
    array = jax.random.normal(own_key, dims, jnp.float32) * deviation
    if len(cuts) > 0:
        array = shard_levels(own_key, dims, cuts, -0.22, 0.18) * array
    return jnp.clip(array, min=-reach, max=reach).astype(kind)


def setup_inputs(seed: int = 0) -> dict:
    streams_of = jax.random.split(jax.random.key(seed), 10)
    return {
        "llama_context": centred(streams_of[0], (PAIRS * TXT, DL), 1.0, 6.0, ((1, 8),)),
        "llama_residual": centred(streams_of[1], (PAIRS * TXT, DL), 1.0, 6.0, ((1, 64),)),
        "w_attn_out": centred(streams_of[2], (DL, DL), DL ** -0.5, 0.09375, ((0, 8), (1, 64))),
        "w_caption": centred(streams_of[3], (DL, D), DL ** -0.5, 0.09375, ((0, 64), (1, 8))),
        "w_text_kv": centred(streams_of[4], (D, 2, HEADS * HD), D ** -0.5, 0.125, ((2, 8),)),
        "prompt_length": draw_prompt_length(jax.random.fold_in(streams_of[9], 71), 0),
        "image_query": draw_image_query(jax.random.fold_in(streams_of[9], 71), 0),
        "image_key": draw_image_key(jax.random.fold_in(streams_of[9], 71), 0),
        "image_value": centred(streams_of[8], (2, PAIRS * IMG, HEADS * HD), 1.0, 6.0, ((1, 64), (2, 8))),
    }


def blocked_sum(left, right, groups):
    block_width = left.shape[1] // groups
    summed = jnp.zeros((left.shape[0], right.shape[1]), jnp.float32)
    for tp_group in range(groups):
        lower_edge = tp_group * block_width
        partial_term = jnp.dot(left[:, lower_edge:lower_edge + block_width], right[lower_edge:lower_edge + block_width], preferred_element_type=jnp.float32)
        rounded = lax.optimization_barrier(partial_term.astype(jnp.bfloat16))
        summed = summed + rounded.astype(jnp.float32)
    return summed

def reference(llama_context, llama_residual, w_attn_out, w_caption, w_text_kv, prompt_length, image_query, image_key, image_value):
    llama_attn = blocked_sum(llama_context, w_attn_out, N_TP)
    llama_hidden = (llama_residual.astype(jnp.float32) + llama_attn).astype(jnp.bfloat16)
    text_states = jnp.dot(llama_hidden, w_caption, preferred_element_type=jnp.float32).astype(jnp.bfloat16)
    text_kv = jnp.einsum('td,djc->tjc', text_states.astype(jnp.float32), w_text_kv.astype(jnp.float32)).astype(jnp.bfloat16)
    scale_factor = 1.0 / math.sqrt(HD)

    def attend(flat_index):
        side_index = flat_index // (PAIRS * HEADS)
        pair_index = flat_index // HEADS % PAIRS
        lead_column = flat_index % HEADS * HD
        anchor = jnp.zeros((), jnp.int32)
        first_row = (pair_index * IMG).astype(jnp.int32)
        queries = lax.dynamic_slice(image_query, (side_index, first_row, lead_column), (1, IMG, HD))[0]
        image_keys = lax.dynamic_slice(image_key, (side_index, first_row, lead_column), (1, IMG, HD))[0]
        image_values = lax.dynamic_slice(image_value, (side_index, first_row, lead_column), (1, IMG, HD))[0]
        text_pair = lax.dynamic_slice(text_kv, ((pair_index * TXT).astype(jnp.int32), anchor, lead_column), (TXT, 2, HD))
        live_text = jnp.arange(TXT, dtype=jnp.int32) < prompt_length[pair_index]
        live_mask = jnp.concatenate([live_text, jnp.ones((IMG,), bool)])
        key_rows = jnp.concatenate([text_pair[:, 0], image_keys], axis=0)
        value_rows = jnp.concatenate([text_pair[:, 1], image_values], axis=0)
        scores = jnp.dot(queries, key_rows.T, preferred_element_type=jnp.float32) * scale_factor
        scores = jnp.where(live_mask[None, :], scores, -1e+30)
        maxima = lax.optimization_barrier(jnp.max(scores, axis=1, keepdims=True))
        weights = jnp.exp(scores - maxima)
        totals = lax.optimization_barrier(jnp.sum(weights, axis=1, keepdims=True))
        mixture = jnp.dot(weights.astype(jnp.bfloat16), value_rows, preferred_element_type=jnp.float32) / totals
        return mixture.astype(jnp.bfloat16)
    heads_out = lax.map(attend, jnp.arange(2 * PAIRS * HEADS, dtype=jnp.int32))
    joint_context = heads_out.reshape(2, PAIRS, HEADS, IMG, HD).transpose(0, 1, 3, 2, 4).reshape(2, PAIRS * IMG, HEADS * HD)
    return joint_context
```

```python
import math

import jax
import jax.numpy as jnp
from jax import lax
from jax.experimental import pallas as pl
from jax.experimental.pallas import tpu as pltpu
from jax.sharding import PartitionSpec as P

TXT = 128
HD = 128
IMG = 4096
NEG = -1e30
BF = jnp.bfloat16
F32 = jnp.float32
SCALE = 1.0 / math.sqrt(HD)

Z_HI = 4
GROUP = 16


def spread(value, axis, groups):
    return lax.all_to_all(value, axis, 0, 0, axis_index_groups=groups)


def seq_groups(chosen):
    return [[p * GROUP + m for m in g] for p in range(Z_HI) for g in chosen]


def member(zlo, y, core):
    return zlo * 8 + y * 2 + core


CHIPS = seq_groups([[member(z, y, c) for z in range(2) for y in range(4)] for c in range(2)])
HALF = seq_groups(
    [[member(z, hf * 2 + y, c) for z in range(2) for y in range(2)] for c in range(2) for hf in range(2)]
)
PAIR = seq_groups([list(range(GROUP))])
ACROSS = [[p * GROUP + m for p in range(Z_HI)] for m in range(GROUP)]
Y_HI = [[2 * x, 2 * x + 1] for x in range(4)]
X_RING = [[2 * x + h for x in range(4)] for h in range(2)]


def image_kernel(q_ref, k0_ref, v0_ref, k1_ref, v1_ref, o_ref, lse_ref):
    q = q_ref[0]
    dims = (((1,), (1,)), ((), ()))

    def scores(ref):
        k = ref[...].reshape(-1, HD)
        return lax.dot_general(q, k, dims, preferred_element_type=F32)

    s0 = scores(k0_ref)
    s1 = scores(k1_ref)
    top = jnp.maximum(jnp.max(s0, axis=1, keepdims=True), jnp.max(s1, axis=1, keepdims=True))
    factor = SCALE * math.log2(math.e)
    shift = top * factor
    p0 = jnp.exp2(s0 * factor - shift)
    p1 = jnp.exp2(s1 * factor - shift)
    total = jnp.sum(p0, axis=1, keepdims=True) + jnp.sum(p1, axis=1, keepdims=True)
    acc = jnp.dot(p0.astype(BF), v0_ref[...].reshape(-1, HD), preferred_element_type=F32)
    acc += jnp.dot(p1.astype(BF), v1_ref[...].reshape(-1, HD), preferred_element_type=F32)
    o_ref[0] = (acc / total).astype(BF)
    lse = top * SCALE + jnp.log(total)
    lse_ref[0] = jnp.transpose(jnp.broadcast_to(lse, (lse.shape[0], HD)))[:8]


def image_attention(q, own, other):
    blocks, rows, _ = q.shape
    chips = own.shape[0]
    kv = lambda j: pl.BlockSpec((chips, None, rows, HD), lambda i: (0, j, 0, 0), pipeline_mode=pl.Buffered(1))
    return pl.pallas_call(
        image_kernel,
        grid=(blocks,),
        in_specs=[pl.BlockSpec((1, rows, HD), lambda i: (i, 0, 0)), kv(0), kv(1), kv(0), kv(1)],
        out_specs=[
            pl.BlockSpec((1, rows, HD), lambda i: (i, 0, 0)),
            pl.BlockSpec((1, 8, rows), lambda i: (i, 0, 0)),
        ],
        out_shape=[
            jax.ShapeDtypeStruct((blocks, rows, HD), BF),
            jax.ShapeDtypeStruct((blocks, 8, rows), F32),
        ],
        name="image_attention",
        compiler_params=pltpu.CompilerParams(vmem_limit_bytes=48 * 1024 * 1024),
    )(q, own, own, other, other)


def text_kernel(live_ref, q_ref, kv_ref, o_ref, lse_ref, out_ref):
    live = live_ref[0]
    kv = kv_ref[...].reshape(TXT, -1)
    heads = q_ref.shape[2] // HD
    for side in range(q_ref.shape[0]):
        for head in range(heads):
            cols = slice(head * HD, (head + 1) * HD)
            unit = side * heads + head
            q = q_ref[side, :, cols]
            k = kv[:, cols]
            v = kv[:, (heads + head) * HD : (heads + head + 1) * HD]
            s = lax.dot_general(q, k, (((1,), (1,)), ((), ())), preferred_element_type=F32) * SCALE
            kept = lax.broadcasted_iota(jnp.int32, s.shape, 1) < live
            s = jnp.where(kept, s, NEG)
            lse = jnp.transpose(lse_ref[unit])[:, :1]
            top = jnp.maximum(jnp.max(s, axis=1, keepdims=True), lse)
            p = jnp.exp(s - top)
            image = jnp.exp(lse - top)
            total = image + jnp.sum(p, axis=1, keepdims=True)
            acc = jnp.dot(p.astype(BF), v, preferred_element_type=F32)
            acc += image * o_ref[unit].astype(F32)
            out_ref[side, :, cols] = (acc / total).astype(BF)


def text_attention(live, q, kv, o, lse):
    full = lambda a: pl.BlockSpec(a.shape, lambda: (0,) * a.ndim)
    return pl.pallas_call(
        text_kernel,
        in_specs=[pl.BlockSpec(memory_space=pltpu.SMEM), full(q), full(kv), full(o), full(lse)],
        out_specs=full(q),
        out_shape=jax.ShapeDtypeStruct(q.shape, BF),
        name="text_attention",
    )(live, q, kv, o, lse)


def local(
    llama_context,
    llama_residual,
    w_attn_out,
    w_caption,
    w_text_kv,
    prompt_length,
    image_query,
    image_key,
    image_value,
):
    sides, rows, width = image_query.shape
    heads = width // HD
    seq_index = lax.axis_index("seq")
    pair = seq_index // GROUP
    live = jnp.sum(
        jnp.where(jnp.arange(prompt_length.shape[0], dtype=jnp.int32) == pair, prompt_length, 0)
    ).reshape(1)

    term = lax.dot_general(
        w_attn_out, llama_context, (((0,), (1,)), ((), ())), preferred_element_type=F32
    ).astype(BF)
    swap = [(t, t ^ 1) for t in range(8)]
    term_far = lax.ppermute(term, "tp", swap)

    def units(a):
        return a.reshape(sides, rows, heads, HD).transpose(0, 2, 1, 3)

    kv = jnp.stack((units(image_key), units(image_value)), axis=2)
    kv = jnp.broadcast_to(kv[:, None], (sides, 2, heads, 2, rows, HD)).reshape(8, 2, rows, HD)
    kv_own = spread(kv, "seq", CHIPS)
    q_own = spread(units(image_query).reshape(4, rows, HD), "seq", HALF)

    cap = jnp.broadcast_to(w_caption[None], (2,) + w_caption.shape)
    cap = spread(cap, "tp", Y_HI)
    cap = jnp.broadcast_to(cap[None], (4,) + cap.shape)
    cap = spread(cap, "tp", X_RING)
    cap = cap.reshape(8, *w_caption.shape).transpose(1, 0, 2).reshape(w_caption.shape[0], -1)
    w_kv = w_text_kv.reshape(w_text_kv.shape[0], -1)
    joint = jnp.dot(cap, w_kv, preferred_element_type=F32).astype(BF)
    joint = spread(jnp.broadcast_to(joint[None], (Z_HI,) + joint.shape), "seq", ACROSS)
    joint = joint.reshape(-1, joint.shape[-1])

    near = (term.astype(F32) + term_far.astype(F32)).astype(BF)
    total = near.astype(F32) + llama_residual.T.astype(F32)
    for step in range(1, 4):
        ring = [(x * 2 + h, (x + step) % 4 * 2 + h) for x in range(4) for h in range(2)]
        total = total + lax.ppermute(near, "tp", ring).astype(F32)
    hidden = total.astype(BF)
    feats = hidden.shape[0]
    hidden = spread(hidden.reshape(feats, Z_HI, TXT).transpose(1, 0, 2), "seq", ACROSS)
    hidden = hidden.reshape(-1, TXT)
    part = lax.dot_general(hidden, joint, (((0,), (0,)), ((), ())), preferred_element_type=F32)
    part = spread(part.astype(BF).reshape(GROUP, TXT // GROUP, -1), "seq", PAIR)
    text = jnp.sum(part.astype(F32), axis=0).astype(BF)
    text = spread(jnp.broadcast_to(text[None], (GROUP,) + text.shape), "seq", PAIR)

    kv_other = lax.ppermute(kv_own, "seq", [(i, i ^ 1) for i in range(64)])
    o_img, lse = image_attention(q_own, kv_own, kv_other)
    o_img = spread(o_img, "seq", HALF)
    lse = spread(lse, "seq", HALF)
    return text_attention(live, image_query, text, o_img, lse)


def solution(mesh):
    placed = (
        P(None, "tp"),
        P(None, "seq"),
        P("tp", "seq"),
        P("seq", "tp"),
        P(None, None, "tp"),
        P(),
        P(None, "seq", "tp"),
        P(None, "seq", "tp"),
        P(None, "seq", "tp"),
    )
    return jax.shard_map(
        local, mesh=mesh, in_specs=placed, out_specs=P(None, "seq", "tp"), check_vma=False
    )
```

```python
import math

import jax
import jax.numpy as jnp
from jax import lax
from jax.experimental import pallas as pl
from jax.experimental.pallas import tpu as pltpu
from jax.sharding import PartitionSpec as P


TXT = 128
HD = 128
NEG = -1e30
BF = jnp.bfloat16
F32 = jnp.float32
SCALE = 1.0 / math.sqrt(HD)
LOG2E = math.log2(math.e)

X, Z_HI, GROUP = 4, 4, 16
CAP = 384
NT = (((1,), (1,)), ((), ()))
TN = (((0,), (0,)), ((), ()))


def spread(value):
    groups = [[p * GROUP + m for m in range(GROUP)] for p in range(Z_HI)]
    return lax.all_to_all(value, "seq", 0, 0, axis_index_groups=groups)


def shifted(value, axis, span, stride, step):
    size = lax.axis_size(axis)
    to = lambda i: i + ((i // stride % span + step) % span - i // stride % span) * stride
    return lax.ppermute(value, axis, [(i, to(i)) for i in range(size)])


KEYS, PIECE = TXT, 64
SENT = 2 * KEYS + PIECE
LSE, TEXT = PIECE, PIECE + 8
BACK = TEXT + 32


def duty(m):
    return m // 8, m // 2 % 2, m % 2, m // 4 % 2 * 2 + m % 2


def call(kernel, args, outs, scalars=0, mib=4, **extra):
    vmem = pl.BlockSpec(memory_space=pltpu.VMEM)
    smem = pl.BlockSpec(memory_space=pltpu.SMEM)
    result = pl.pallas_call(
        kernel,
        in_specs=[smem] * scalars + [vmem] * (len(args) - scalars),
        out_specs=[vmem] * len(outs),
        out_shape=outs,
        compiler_params=pltpu.CompilerParams(vmem_limit_bytes=mib << 20),
        **extra,
    )(*args)
    return result[0] if len(outs) == 1 else result


def after(value, *others):
    return lax.optimization_barrier((value, *others))[0]


def shape(*dims, dtype=BF):
    return jax.ShapeDtypeStruct(dims, dtype)


def project_kernel(ctx_ref, w_ref, cap_ref, out_ref):
    term = lax.dot_general(w_ref[...], ctx_ref[...], NT, preferred_element_type=F32)
    rows = term.shape[1]
    out_ref[:, :rows] = term.astype(BF)
    out_ref[:, rows : rows + cap_ref.shape[1]] = cap_ref[...]
    out_ref[:, rows + cap_ref.shape[1] :] = jnp.zeros_like(out_ref[:, rows + cap_ref.shape[1] :])


def near_kernel(own_ref, far_ref, out_ref):
    rows = own_ref.shape[1] - CAP
    out_ref[:, :rows] = (own_ref[:, :rows].astype(F32) + far_ref[:, :rows].astype(F32)).astype(BF)
    out_ref[:, rows : rows + CAP] = own_ref[:, rows:]
    out_ref[:, rows + CAP :] = far_ref[:, rows:]


def joint_kernel(pos_ref, n0, n1, n2, n3, res_ref, w_ref, o0, o1, o2, o3, hid_ref):
    x, yhi, zhi = pos_ref[0], pos_ref[1], pos_ref[2]
    rows = hid_ref.shape[1]
    cols = w_ref.shape[0] // (2 * X)
    total = res_ref[...].astype(F32)
    joint = jnp.zeros((total.shape[0], w_ref.shape[1]), F32)
    for step, ref in enumerate((n0, n1, n2, n3)):
        total = total + ref[:, :rows].astype(F32)
        source = (x + X - step) % X
        for far in range(2):
            block = source * 2 + (yhi + far) % 2
            first = pl.multiple_of(block * cols, cols)
            cap = ref[:, rows + far * CAP : rows + far * CAP + cols]
            joint += jnp.dot(cap, w_ref[pl.ds(first, cols), :], preferred_element_type=F32)
    hid_ref[...] = total.astype(BF)
    joint = joint.astype(BF)
    for step, ref in enumerate((o0, o1, o2, o3)):
        first = pl.multiple_of((zhi + step) % Z_HI * TXT, TXT)
        ref[:, :TXT] = hid_ref[:, pl.ds(first, TXT)]
        ref[:, TXT:] = joint


def part_kernel(g0, g1, g2, g3, out_ref):
    part = None
    for ref in (g0, g1, g2, g3):
        term = lax.dot_general(ref[:, :TXT], ref[:, TXT:], TN, preferred_element_type=F32)
        part = term if part is None else part + term
    out_ref[...] = part.astype(BF).reshape(out_ref.shape)


def sum_kernel(part_ref, o_ref, out_ref):
    total = jnp.sum(part_ref[...].astype(F32), axis=0)
    text = jnp.concatenate([total[:, i * HD : (i + 1) * HD] for i in range(4)], axis=0).astype(BF)
    for m in range(GROUP):
        out_ref[m, :TEXT] = o_ref[m]
        out_ref[m, TEXT:] = text


def pack_kernel(_, k_ref, v_ref, q_ref, out_ref):
    for m in range(GROUP):
        side, head, keys, piece = duty(m)
        cols = slice(head * HD, (head + 1) * HD)
        out_ref[m, :KEYS] = k_ref[side, keys * KEYS : (keys + 1) * KEYS, cols]
        out_ref[m, KEYS : 2 * KEYS] = v_ref[side, keys * KEYS : (keys + 1) * KEYS, cols]
        out_ref[m, 2 * KEYS :] = q_ref[side, piece * PIECE : (piece + 1) * PIECE, cols]


def image_kernel(own_ref, other_ref, out_ref):
    for block in range(4):
        members = slice(block * 4, block * 4 + 4)
        q = own_ref[members, 2 * KEYS :].reshape(-1, HD)
        s = [
            lax.dot_general(q, ref[:, :KEYS].reshape(-1, HD), NT, preferred_element_type=F32)
            for ref in (own_ref, other_ref)
        ]
        top = jnp.maximum(*(jnp.max(t, axis=1, keepdims=True) for t in s))
        p = [jnp.exp2(t * (SCALE * LOG2E) - top * (SCALE * LOG2E)) for t in s]
        total = sum(jnp.sum(t, axis=1, keepdims=True) for t in p)
        acc = sum(
            jnp.dot(t.astype(BF), ref[:, KEYS : 2 * KEYS].reshape(-1, HD), preferred_element_type=F32)
            for t, ref in zip(p, (own_ref, other_ref), strict=True)
        )
        out_ref[members, :PIECE] = (acc / total).astype(BF).reshape(4, PIECE, HD)
        rest = top * SCALE + jnp.log(total)
        rest = jnp.transpose(jnp.broadcast_to(rest, (q.shape[0], HD)))[:8]
        first = rest.astype(BF).astype(F32)
        rest = rest - first
        second = rest.astype(BF).astype(F32)
        place = lax.broadcasted_iota(jnp.int32, rest.shape, 0)
        lse = jnp.where(place == 0, first, jnp.where(place == 1, second, rest - second))
        for i in range(4):
            row = jnp.concatenate([lse[:, i * PIECE : (i + 1) * PIECE]] * 2, axis=1)
            out_ref[block * 4 + i, LSE:TEXT] = row.astype(BF)


def text_kernel(pair_ref, live_ref, q_ref, back_ref, out_ref):
    live = live_ref[pair_ref[0]]
    text = [
        back_ref[:, TEXT + 8 * i : TEXT + 8 * i + 8].astype(F32).reshape(TXT, HD).astype(BF) for i in range(4)
    ]
    kept = lax.broadcasted_iota(jnp.int32, (PIECE, TXT), 1) < live
    for m in range(GROUP):
        side, head, _, piece = duty(m)
        place = (side, slice(piece * PIECE, (piece + 1) * PIECE), slice(head * HD, (head + 1) * HD))
        s = lax.dot_general(q_ref[place], text[head], NT, preferred_element_type=F32) * SCALE
        s = jnp.where(kept, s, NEG)
        tail = back_ref[m, LSE:TEXT].astype(F32)
        lse = jnp.broadcast_to(tail[:1] + tail[1:2] + tail[2:3], tail.shape)
        lse = jnp.transpose(lse)[:PIECE, :1]
        top = jnp.maximum(jnp.max(s, axis=1, keepdims=True), lse)
        p = jnp.exp(s - top)
        image = jnp.exp(lse - top)
        total = image + jnp.sum(p, axis=1, keepdims=True)
        acc = jnp.dot(p.astype(BF), text[2 + head], preferred_element_type=F32)
        acc += image * back_ref[m, :PIECE].astype(F32)
        out_ref[place] = (acc / total).astype(BF)


def local(
    llama_context,
    llama_residual,
    w_attn_out,
    w_caption,
    w_text_kv,
    prompt_length,
    image_query,
    image_key,
    image_value,
):
    tp, seq = lax.axis_index("tp"), lax.axis_index("seq")
    pos = jnp.stack((tp >> 1, tp & 1, seq >> 4))
    feats, text_rows = w_attn_out.shape[1], llama_context.shape[0]
    w_kv = w_text_kv.reshape(w_text_kv.shape[0], -1)
    kv_cols = w_kv.shape[1]

    term = call(project_kernel, (llama_context, w_attn_out.T, w_caption), [shape(feats, text_rows + CAP)])
    far = lax.ppermute(term, "tp", [(t, t ^ 1) for t in range(2 * X)])
    own = call(pack_kernel, (term, image_key, image_value, image_query), [shape(GROUP, SENT, HD)])
    own = spread(own)

    near = call(near_kernel, (term, far), [shape(feats, text_rows + 2 * CAP)])
    ring = [near] + [shifted(near, "tp", X, 2, step) for step in range(1, X)]
    sends = call(
        joint_kernel,
        (pos, *ring, llama_residual.T, w_kv),
        [shape(feats, TXT + kv_cols)] * Z_HI,
        scalars=1,
        mib=8,
        scratch_shapes=[pltpu.VMEM((feats, text_rows), BF)],
    )
    parts = [sends[0]] + [shifted(sends[step], "seq", Z_HI, GROUP, step) for step in range(1, Z_HI)]
    part = call(part_kernel, parts, [shape(GROUP, TXT // GROUP, kv_cols)])

    part, own = lax.optimization_barrier((part, own))
    other = lax.ppermute(own, "seq", [(i, i ^ 1) for i in range(Z_HI * GROUP)])
    part = spread(part)
    o = call(image_kernel, (own, other), [shape(GROUP, TEXT, HD)], mib=32)
    back = call(sum_kernel, (after(part, o), o), [shape(GROUP, BACK, HD)])
    back = spread(back)
    return call(text_kernel, (pos[2:], prompt_length, image_query, back), [shape(*image_query.shape)], scalars=2)


def solution(mesh):
    placed = (
        P(None, "tp"),
        P(None, "seq"),
        P("tp", "seq"),
        P("seq", "tp"),
        P(None, None, "tp"),
        P(),
        P(None, "seq", "tp"),
        P(None, "seq", "tp"),
        P(None, "seq", "tp"),
    )

    return jax.shard_map(local, mesh=mesh, in_specs=placed, out_specs=P(None, "seq", "tp"), check_vma=False)
```

```python
import math

import jax
import jax.numpy as jnp
from jax import lax
from jax.experimental import pallas as pl
from jax.experimental.pallas import tpu as pltpu
from jax.sharding import PartitionSpec as P


TXT = 128
HD = 128
NEG = -1e30
BF = jnp.bfloat16
F32 = jnp.float32
SCALE = 1.0 / math.sqrt(HD)
LOG2E = math.log2(math.e)

X, Z_HI, GROUP = 4, 4, 16
NT = (((1,), (1,)), ((), ()))
TN = (((0,), (0,)), ((), ()))


def spread(value):
    groups = [[p * GROUP + m for m in range(GROUP)] for p in range(Z_HI)]
    return lax.all_to_all(value, "seq", 0, 0, axis_index_groups=groups)


def shifted(value, axis, span, stride, step):
    size = lax.axis_size(axis)
    to = lambda i: i + ((i // stride % span + step) % span - i // stride % span) * stride
    return lax.ppermute(value, axis, [(i, to(i)) for i in range(size)])


KEYS, PIECE = TXT, 64
SENT = 2 * KEYS + PIECE
LSE, TEXT = PIECE, PIECE + 8
BACK = TEXT + 32


def duty(m):
    return m // 8, m // 2 % 2, m % 2, m // 4 % 2 * 2 + m % 2


def call(kernel, args, outs, scalars=0, mib=4, hbm=0, hbm_outs=0, **extra):
    vmem = pl.BlockSpec(memory_space=pltpu.VMEM)
    smem = pl.BlockSpec(memory_space=pltpu.SMEM)
    far = pl.BlockSpec(memory_space=pltpu.HBM)
    result = pl.pallas_call(
        kernel,
        in_specs=[smem] * scalars + [far] * hbm + [vmem] * (len(args) - scalars - hbm),
        out_specs=[far] * hbm_outs + [vmem] * (len(outs) - hbm_outs),
        out_shape=outs,
        compiler_params=pltpu.CompilerParams(vmem_limit_bytes=mib << 20),
        **extra,
    )(*args)
    return result[0] if len(outs) == 1 else result


def after(value, *others):
    return lax.optimization_barrier((value, *others))[0]


def shape(*dims, dtype=BF):
    return jax.ShapeDtypeStruct(dims, dtype)


def start_kernel(k_hbm, v_hbm, q_hbm, ctx_hbm, w_hbm, cap_hbm, image_hbm, out_ref, k_ref, v_ref, q_ref, ctx_ref, w_ref, cap_ref, image_ref, sems):
    loads = [
        pltpu.make_async_copy(source, target, sems.at[i])
        for i, (source, target) in enumerate(
            ((k_hbm, k_ref), (v_hbm, v_ref), (q_hbm, q_ref), (ctx_hbm, ctx_ref), (w_hbm, w_ref), (cap_hbm, cap_ref))
        )
    ]
    for load in loads:
        load.start()
    for load in loads[:3]:
        load.wait()
    moves = []
    for m in range(GROUP):
        side, head, keys, piece = duty(m)
        cols = slice(head * HD, (head + 1) * HD)
        rows = slice(keys * KEYS, (keys + 1) * KEYS)
        image_ref[m, :KEYS] = k_ref[side, rows, cols]
        image_ref[m, KEYS : 2 * KEYS] = v_ref[side, rows, cols]
        image_ref[m, 2 * KEYS :] = q_ref[side, piece * PIECE : (piece + 1) * PIECE, cols]
        moves.append(pltpu.make_async_copy(image_ref.at[m], image_hbm.at[m], sems.at[len(loads) + m]))
        moves[-1].start()
    for load in loads[3:]:
        load.wait()
    term = lax.dot_general(w_ref[...], ctx_ref[...], NT, preferred_element_type=F32)
    rows = term.shape[1]
    out_ref[:, :rows] = term.astype(BF)
    out_ref[:, rows:] = cap_ref[...]
    for move in moves:
        move.wait()


def near_kernel(own_ref, far_ref, out_ref):
    cols = (out_ref.shape[1] - own_ref.shape[1])
    rows = own_ref.shape[1] - cols
    out_ref[:, :rows] = (own_ref[:, :rows].astype(F32) + far_ref[:, :rows].astype(F32)).astype(BF)
    out_ref[:, rows:] = jnp.concatenate([own_ref[:, rows:], far_ref[:, rows:]], axis=1)


def joint_kernel(pos_ref, n0, n1, n2, n3, res_ref, w_ref, o0, o1, o2, o3, hid_ref):
    x, yhi, zhi = pos_ref[0], pos_ref[1], pos_ref[2]
    rows = hid_ref.shape[1]
    cols = w_ref.shape[0] // (2 * X)
    total = res_ref[...].astype(F32)
    joint = jnp.zeros((total.shape[0], w_ref.shape[1]), F32)
    for step, ref in enumerate((n0, n1, n2, n3)):
        total = total + ref[:, :rows].astype(F32)
        source = (x + X - step) % X
        for far in range(2):
            block = source * 2 + (yhi + far) % 2
            first = pl.multiple_of(block * cols, cols)
            cap = ref[:, rows + far * cols : rows + (far + 1) * cols]
            joint += jnp.dot(cap, w_ref[pl.ds(first, cols), :], preferred_element_type=F32)
    hid_ref[...] = total.astype(BF)
    joint = joint.astype(BF)
    for step, ref in enumerate((o0, o1, o2, o3)):
        first = pl.multiple_of((zhi + step) % Z_HI * TXT, TXT)
        ref[:, :TXT] = hid_ref[:, pl.ds(first, TXT)]
        ref[:, TXT:] = joint


def part_kernel(g0, g1, g2, g3, out_ref):
    part = None
    for ref in (g0, g1, g2, g3):
        term = lax.dot_general(ref[:, :TXT], ref[:, TXT:], TN, preferred_element_type=F32)
        part = term if part is None else part + term
    out_ref[...] = part.astype(BF).reshape(out_ref.shape)


def sum_kernel(part_ref, o_ref, out_ref):
    total = jnp.sum(part_ref[...].astype(F32), axis=0)
    text = jnp.concatenate([total[:, i * HD : (i + 1) * HD] for i in range(4)], axis=0).astype(BF)
    for m in range(GROUP):
        out_ref[m, :TEXT] = o_ref[m]
        out_ref[m, TEXT:] = text


BLOCK = 512


def image_kernel(own_ref, other_ref, out_ref):
    scale = SCALE * LOG2E
    count = BLOCK // PIECE
    for block in range(GROUP // count):
        members = slice(block * count, (block + 1) * count)
        q = own_ref[members, 2 * KEYS :].reshape(BLOCK, HD)
        top, total, acc = jnp.full((BLOCK, 1), NEG, F32), 0.0, 0.0
        for ref in (own_ref, other_ref):
            s = lax.dot_general(q, ref[:, :KEYS].reshape(-1, HD), NT, preferred_element_type=F32)
            old, top = top, jnp.maximum(top, jnp.max(s, axis=1, keepdims=True))
            p = jnp.exp2(s * scale - top * scale)
            factor = jnp.exp2(old * scale - top * scale)
            values = ref[:, KEYS : 2 * KEYS].reshape(-1, HD)
            total = total * factor + jnp.sum(p, axis=1, keepdims=True)
            acc = acc * factor + jnp.dot(p.astype(BF), values, preferred_element_type=F32)
        out_ref[members, :PIECE] = (acc / total).astype(BF).reshape(count, PIECE, HD)
        rest = top * SCALE + jnp.log(total)
        rest = jnp.transpose(jnp.broadcast_to(rest, (BLOCK, HD)))[:8]
        first = rest.astype(BF).astype(F32)
        rest = rest - first
        second = rest.astype(BF).astype(F32)
        place = lax.broadcasted_iota(jnp.int32, rest.shape, 0)
        lse = jnp.where(place == 0, first, jnp.where(place == 1, second, rest - second))
        for i in range(count):
            row = jnp.concatenate([lse[:, i * PIECE : (i + 1) * PIECE]] * 2, axis=1)
            out_ref[block * count + i, LSE:TEXT] = row.astype(BF)


def text_kernel(pair_ref, live_ref, q_ref, back_ref, out_ref):
    live = live_ref[pair_ref[0]]
    text = [
        back_ref[:, TEXT + 8 * i : TEXT + 8 * i + 8].astype(F32).reshape(TXT, HD).astype(BF) for i in range(4)
    ]
    rows = q_ref.shape[1]
    kept = lax.broadcasted_iota(jnp.int32, (rows, TXT), 1) < live
    low = lax.broadcasted_iota(jnp.int32, (8, HD), 1) < PIECE
    for side in range(2):
        for head in range(2):
            owners = sorted((m for m in range(GROUP) if duty(m)[:2] == (side, head)), key=lambda m: duty(m)[3])
            cols = slice(head * HD, (head + 1) * HD)
            s = lax.dot_general(q_ref[side, :, cols], text[head], NT, preferred_element_type=F32) * SCALE
            s = jnp.where(kept, s, NEG)
            lse = []
            for m in owners:
                tail = back_ref[m, LSE:TEXT].astype(F32)
                lse.append(jnp.broadcast_to(tail[:1] + tail[1:2] + tail[2:3], tail.shape))
            lse = jnp.concatenate([jnp.where(low, lse[0], lse[1]), jnp.where(low, lse[2], lse[3])], axis=1)
            lse = jnp.transpose(lse)[:, :1]
            top = jnp.maximum(jnp.max(s, axis=1, keepdims=True), lse)
            p = jnp.exp(s - top)
            image = jnp.exp(lse - top)
            total = image + jnp.sum(p, axis=1, keepdims=True)
            acc = jnp.dot(p.astype(BF), text[2 + head], preferred_element_type=F32)
            acc += image * jnp.concatenate([back_ref[m, :PIECE] for m in owners], axis=0).astype(F32)
            out_ref[side, :, cols] = (acc / total).astype(BF)


def local(
    llama_context,
    llama_residual,
    w_attn_out,
    w_caption,
    w_text_kv,
    prompt_length,
    image_query,
    image_key,
    image_value,
):
    tp, seq = lax.axis_index("tp"), lax.axis_index("seq")
    pos = jnp.stack((tp >> 1, tp & 1, seq >> 4))
    feats, text_rows = w_attn_out.shape[1], llama_context.shape[0]
    w_kv = w_text_kv.reshape(w_text_kv.shape[0], -1)
    kv_cols = w_kv.shape[1]

    cap_cols = w_caption.shape[1]
    image, term = call(
        start_kernel,
        (image_key, image_value, image_query, llama_context, w_attn_out.T, w_caption),
        [shape(GROUP, SENT, HD), shape(feats, text_rows + cap_cols)],
        mib=60,
        hbm=6,
        hbm_outs=1,
        scratch_shapes=[
            *[pltpu.VMEM(image_query.shape, BF)] * 3,
            pltpu.VMEM(llama_context.shape, BF),
            pltpu.VMEM(w_attn_out.shape[::-1], BF),
            pltpu.VMEM(w_caption.shape, BF),
            pltpu.VMEM((GROUP, SENT, HD), BF),
            pltpu.SemaphoreType.DMA((6 + GROUP,)),
        ],
    )
    far = lax.ppermute(term, "tp", [(t, t ^ 1) for t in range(2 * X)])
    own = spread(image)

    near = call(near_kernel, (term, far), [shape(feats, text_rows + 2 * cap_cols)])
    ring = [near] + [shifted(near, "tp", X, 2, step) for step in range(1, X)]
    sends = call(
        joint_kernel,
        (pos, *ring, llama_residual.T, w_kv),
        [shape(feats, TXT + kv_cols)] * Z_HI,
        scalars=1,
        mib=8,
        scratch_shapes=[pltpu.VMEM((feats, text_rows), BF)],
    )
    parts = [sends[0]] + [shifted(sends[step], "seq", Z_HI, GROUP, step) for step in range(1, Z_HI)]
    own = after(own, sends[0])
    other = lax.ppermute(own, "seq", [(i, i ^ 1) for i in range(Z_HI * GROUP)])
    part = call(part_kernel, parts, [shape(GROUP, TXT // GROUP, kv_cols)])
    part = spread(part)
    o = call(image_kernel, (own, other), [shape(GROUP, TEXT, HD)], mib=32)
    back = call(sum_kernel, (after(part, o), o), [shape(GROUP, BACK, HD)])
    back = spread(back)
    return call(text_kernel, (pos[2:], prompt_length, image_query, back), [shape(*image_query.shape)], scalars=2)


def solution(mesh):
    placed = (
        P(None, "tp"),
        P(None, "seq"),
        P("tp", "seq"),
        P("seq", "tp"),
        P(None, None, "tp"),
        P(),
        P(None, "seq", "tp"),
        P(None, "seq", "tp"),
        P(None, "seq", "tp"),
    )

    return jax.shard_map(local, mesh=mesh, in_specs=placed, out_specs=P(None, "seq", "tp"), check_vma=False)
```

```python
import math

import jax
import jax.numpy as jnp
from jax import lax
from jax.experimental import pallas as pl
from jax.experimental.pallas import tpu as pltpu
from jax.sharding import PartitionSpec as P


TXT = 128
HD = 128
NEG = -1e30
BF = jnp.bfloat16
F32 = jnp.float32
SCALE = 1.0 / math.sqrt(HD)
LOG2E = math.log2(math.e)

X, Z_HI, GROUP = 4, 4, 16
NT = (((1,), (1,)), ((), ()))
TN = (((0,), (0,)), ((), ()))


def spread(value):
    groups = [[p * GROUP + m for m in range(GROUP)] for p in range(Z_HI)]
    return lax.all_to_all(value, "seq", 0, 0, axis_index_groups=groups)


def shifted(value, axis, span, stride, step):
    size = lax.axis_size(axis)
    to = lambda i: i + ((i // stride % span + step) % span - i // stride % span) * stride
    return lax.ppermute(value, axis, [(i, to(i)) for i in range(size)])


KEYS, PIECE = TXT, 64
SENT = 2 * KEYS + PIECE
LSE, TEXT = PIECE, PIECE + 8
BACK = TEXT + 32


def duty(m):
    return m // 8, m // 2 % 2, m % 2, m // 4 % 2 * 2 + m % 2


def call(kernel, args, outs, scalars=0, mib=4, hbm=0, hbm_outs=0, **extra):
    vmem = pl.BlockSpec(memory_space=pltpu.VMEM)
    smem = pl.BlockSpec(memory_space=pltpu.SMEM)
    far = pl.BlockSpec(memory_space=pltpu.HBM)
    result = pl.pallas_call(
        kernel,
        in_specs=[smem] * scalars + [far] * hbm + [vmem] * (len(args) - scalars - hbm),
        out_specs=[far] * hbm_outs + [vmem] * (len(outs) - hbm_outs),
        out_shape=outs,
        compiler_params=pltpu.CompilerParams(vmem_limit_bytes=mib << 20),
        **extra,
    )(*args)
    return result[0] if len(outs) == 1 else result


def after(value, *others):
    return lax.optimization_barrier((value, *others))[0]


def shape(*dims, dtype=BF):
    return jax.ShapeDtypeStruct(dims, dtype)


def start_kernel(k_hbm, v_hbm, q_hbm, ctx_hbm, w_hbm, cap_hbm, image_hbm, out_ref, k_ref, v_ref, q_ref, ctx_ref, w_ref, cap_ref, image_ref, sems):
    loads = [
        pltpu.make_async_copy(source, target, sems.at[i])
        for i, (source, target) in enumerate(
            ((k_hbm, k_ref), (v_hbm, v_ref), (q_hbm, q_ref), (ctx_hbm, ctx_ref), (w_hbm, w_ref), (cap_hbm, cap_ref))
        )
    ]
    for load in loads:
        load.start()
    for load in loads[:3]:
        load.wait()
    moves = []
    for m in range(GROUP):
        side, head, keys, piece = duty(m)
        cols = slice(head * HD, (head + 1) * HD)
        rows = slice(keys * KEYS, (keys + 1) * KEYS)
        image_ref[m, :KEYS] = k_ref[side, rows, cols]
        image_ref[m, KEYS : 2 * KEYS] = v_ref[side, rows, cols]
        image_ref[m, 2 * KEYS :] = q_ref[side, piece * PIECE : (piece + 1) * PIECE, cols]
        moves.append(pltpu.make_async_copy(image_ref.at[m], image_hbm.at[m], sems.at[len(loads) + m]))
        moves[-1].start()
    for load in loads[3:]:
        load.wait()
    term = lax.dot_general(w_ref[...], ctx_ref[...], NT, preferred_element_type=F32)
    rows = term.shape[1]
    out_ref[:, :rows] = term.astype(BF)
    out_ref[:, rows:] = cap_ref[...]
    for move in moves:
        move.wait()


def near_kernel(own_ref, far_ref, out_ref):
    cols = (out_ref.shape[1] - own_ref.shape[1])
    rows = own_ref.shape[1] - cols
    out_ref[:, :rows] = (own_ref[:, :rows].astype(F32) + far_ref[:, :rows].astype(F32)).astype(BF)
    out_ref[:, rows:] = jnp.concatenate([own_ref[:, rows:], far_ref[:, rows:]], axis=1)


def joint_kernel(pos_ref, n0, n1, n2, n3, res_ref, w_ref, o0, o1, o2, o3, hid_ref):
    x, yhi, zhi = pos_ref[0], pos_ref[1], pos_ref[2]
    rows = hid_ref.shape[1]
    cols = w_ref.shape[0] // (2 * X)
    total = res_ref[...].astype(F32)
    joint = jnp.zeros((total.shape[0], w_ref.shape[1]), F32)
    for step, ref in enumerate((n0, n1, n2, n3)):
        total = total + ref[:, :rows].astype(F32)
        source = (x + X - step) % X
        for far in range(2):
            block = source * 2 + (yhi + far) % 2
            first = pl.multiple_of(block * cols, cols)
            cap = ref[:, rows + far * cols : rows + (far + 1) * cols]
            joint += jnp.dot(cap, w_ref[pl.ds(first, cols), :], preferred_element_type=F32)
    hid_ref[...] = total.astype(BF)
    joint = joint.astype(BF)
    for step, ref in enumerate((o0, o1, o2, o3)):
        first = pl.multiple_of((zhi + step) % Z_HI * TXT, TXT)
        ref[:, :TXT] = hid_ref[:, pl.ds(first, TXT)]
        ref[:, TXT:] = joint


def part_kernel(g0, g1, g2, g3, out_ref):
    part = None
    for ref in (g0, g1, g2, g3):
        term = lax.dot_general(ref[:, :TXT], ref[:, TXT:], TN, preferred_element_type=F32)
        part = term if part is None else part + term
    out_ref[...] = part.astype(BF).reshape(out_ref.shape)


def sum_kernel(part_ref, o_ref, out_ref):
    total = jnp.sum(part_ref[...].astype(F32), axis=0)
    text = jnp.concatenate([total[:, i * HD : (i + 1) * HD] for i in range(4)], axis=0).astype(BF)
    for m in range(GROUP):
        out_ref[m, :TEXT] = o_ref[m]
        out_ref[m, TEXT:] = text


BLOCK = 512


def image_kernel(own_ref, other_ref, out_ref):
    scale = SCALE * LOG2E
    count = BLOCK // PIECE
    for block in range(GROUP // count):
        members = slice(block * count, (block + 1) * count)
        q = own_ref[members, 2 * KEYS :].reshape(BLOCK, HD)
        top, total, acc = jnp.full((BLOCK, 1), NEG, F32), 0.0, 0.0
        for ref in (own_ref, other_ref):
            s = lax.dot_general(q, ref[:, :KEYS].reshape(-1, HD), NT, preferred_element_type=F32)
            old, top = top, jnp.maximum(top, jnp.max(s, axis=1, keepdims=True))
            p = jnp.exp2(s * scale - top * scale)
            factor = jnp.exp2(old * scale - top * scale)
            values = ref[:, KEYS : 2 * KEYS].reshape(-1, HD)
            total = total * factor + jnp.sum(p, axis=1, keepdims=True)
            acc = acc * factor + jnp.dot(p.astype(BF), values, preferred_element_type=F32)
        out_ref[members, :PIECE] = (acc / total).astype(BF).reshape(count, PIECE, HD)
        rest = top * SCALE + jnp.log(total)
        rest = jnp.transpose(jnp.broadcast_to(rest, (BLOCK, HD)))[:8]
        first = rest.astype(BF).astype(F32)
        rest = rest - first
        second = rest.astype(BF).astype(F32)
        place = lax.broadcasted_iota(jnp.int32, rest.shape, 0)
        lse = jnp.where(place == 0, first, jnp.where(place == 1, second, rest - second))
        for i in range(count):
            row = jnp.concatenate([lse[:, i * PIECE : (i + 1) * PIECE]] * 2, axis=1)
            out_ref[block * count + i, LSE:TEXT] = row.astype(BF)


def text_kernel(pair_ref, live_ref, q_ref, back_ref, out_hbm, out_ref, sems):
    live = live_ref[pair_ref[0]]
    text = [
        back_ref[:, TEXT + 8 * i : TEXT + 8 * i + 8].astype(F32).reshape(TXT, HD).astype(BF) for i in range(4)
    ]
    rows = q_ref.shape[1]
    kept = lax.broadcasted_iota(jnp.int32, (rows, TXT), 1) < live
    low = lax.broadcasted_iota(jnp.int32, (8, HD), 1) < PIECE
    stores = []
    for side in range(2):
        for head in range(2):
            owners = sorted((m for m in range(GROUP) if duty(m)[:2] == (side, head)), key=lambda m: duty(m)[3])
            cols = slice(head * HD, (head + 1) * HD)
            s = lax.dot_general(q_ref[side, :, cols], text[head], NT, preferred_element_type=F32) * SCALE
            s = jnp.where(kept, s, NEG)
            lse = []
            for m in owners:
                tail = back_ref[m, LSE:TEXT].astype(F32)
                lse.append(jnp.broadcast_to(tail[:1] + tail[1:2] + tail[2:3], tail.shape))
            lse = jnp.concatenate([jnp.where(low, lse[0], lse[1]), jnp.where(low, lse[2], lse[3])], axis=1)
            lse = jnp.transpose(lse)[:, :1]
            top = jnp.maximum(jnp.max(s, axis=1, keepdims=True), lse)
            p = jnp.exp(s - top)
            image = jnp.exp(lse - top)
            total = image + jnp.sum(p, axis=1, keepdims=True)
            acc = jnp.dot(p.astype(BF), text[2 + head], preferred_element_type=F32)
            acc += image * jnp.concatenate([back_ref[m, :PIECE] for m in owners], axis=0).astype(F32)
            out_ref[side, :, cols] = (acc / total).astype(BF)
        stores.append(pltpu.make_async_copy(out_ref.at[side], out_hbm.at[side], sems.at[side]))
        stores[-1].start()
    for store in stores:
        store.wait()


def local(
    llama_context,
    llama_residual,
    w_attn_out,
    w_caption,
    w_text_kv,
    prompt_length,
    image_query,
    image_key,
    image_value,
):
    tp, seq = lax.axis_index("tp"), lax.axis_index("seq")
    pos = jnp.stack((tp >> 1, tp & 1, seq >> 4))
    feats, text_rows = w_attn_out.shape[1], llama_context.shape[0]
    w_kv = w_text_kv.reshape(w_text_kv.shape[0], -1)
    kv_cols = w_kv.shape[1]

    cap_cols = w_caption.shape[1]
    image, term = call(
        start_kernel,
        (image_key, image_value, image_query, llama_context, w_attn_out.T, w_caption),
        [shape(GROUP, SENT, HD), shape(feats, text_rows + cap_cols)],
        mib=60,
        hbm=6,
        hbm_outs=1,
        scratch_shapes=[
            *[pltpu.VMEM(image_query.shape, BF)] * 3,
            pltpu.VMEM(llama_context.shape, BF),
            pltpu.VMEM(w_attn_out.shape[::-1], BF),
            pltpu.VMEM(w_caption.shape, BF),
            pltpu.VMEM((GROUP, SENT, HD), BF),
            pltpu.SemaphoreType.DMA((6 + GROUP,)),
        ],
    )
    far = lax.ppermute(term, "tp", [(t, t ^ 1) for t in range(2 * X)])
    own = spread(image)

    near = call(near_kernel, (term, far), [shape(feats, text_rows + 2 * cap_cols)])
    ring = [near]
    for step in range(1, X):
        ring.append(shifted(near, "tp", X, 2, step))
    sends = call(
        joint_kernel,
        (pos, *ring, llama_residual.T, w_kv),
        [shape(feats, TXT + kv_cols)] * Z_HI,
        scalars=1,
        mib=8,
        scratch_shapes=[pltpu.VMEM((feats, text_rows), BF)],
    )
    parts = [sends[0]]
    for step in range(1, Z_HI):
        parts.append(shifted(sends[step], "seq", Z_HI, GROUP, step))
    own = after(own, sends[0])
    other = lax.ppermute(own, "seq", [(i, i ^ 1) for i in range(Z_HI * GROUP)])
    part = call(part_kernel, parts, [shape(GROUP, TXT // GROUP, kv_cols)])
    part = spread(part)
    o = call(image_kernel, (own, other), [shape(GROUP, TEXT, HD)], mib=32)
    back = call(sum_kernel, (after(part, o), o), [shape(GROUP, BACK, HD)])
    back = spread(back)
    return call(
        text_kernel,
        (pos[2:], prompt_length, image_query, back),
        [shape(*image_query.shape)],
        scalars=2,
        hbm_outs=1,
        scratch_shapes=[pltpu.VMEM(image_query.shape, BF), pltpu.SemaphoreType.DMA((image_query.shape[0],))],
    )


def solution(mesh):
    placed = (
        P(None, "tp"),
        P(None, "seq"),
        P("tp", "seq"),
        P("seq", "tp"),
        P(None, None, "tp"),
        P(),
        P(None, "seq", "tp"),
        P(None, "seq", "tp"),
        P(None, "seq", "tp"),
    )

    return jax.shard_map(local, mesh=mesh, in_specs=placed, out_specs=P(None, "seq", "tp"), check_vma=False)
```

```python
import math

import jax
import jax.numpy as jnp
from jax import lax
from jax.experimental import pallas as pl
from jax.experimental.pallas import tpu as pltpu
from jax.sharding import PartitionSpec as P


TXT = 128
HD = 128
NEG = -1e30
BF = jnp.bfloat16
F32 = jnp.float32
SCALE = 1.0 / math.sqrt(HD)
LOG2E = math.log2(math.e)

X, Z_HI, GROUP = 4, 4, 16
NT = (((1,), (1,)), ((), ()))
TN = (((0,), (0,)), ((), ()))


def spread(value):
    groups = [[p * GROUP + m for m in range(GROUP)] for p in range(Z_HI)]
    return lax.all_to_all(value, "seq", 0, 0, axis_index_groups=groups)


def shifted(value, axis, span, stride, step):
    size = lax.axis_size(axis)
    to = lambda i: i + ((i // stride % span + step) % span - i // stride % span) * stride
    return lax.ppermute(value, axis, [(i, to(i)) for i in range(size)])


KEYS, PIECE = TXT, 64
SENT = 2 * KEYS + PIECE
LSE, TEXT = PIECE, PIECE + 8
BACK = TEXT + 32


def duty(m):
    return m // 8, m // 2 % 2, m % 2, m // 4 % 2 * 2 + m % 2


def call(kernel, args, outs, scalars=0, mib=4, hbm=0, hbm_outs=0, **extra):
    vmem = pl.BlockSpec(memory_space=pltpu.VMEM)
    smem = pl.BlockSpec(memory_space=pltpu.SMEM)
    far = pl.BlockSpec(memory_space=pltpu.HBM)
    result = pl.pallas_call(
        kernel,
        in_specs=[smem] * scalars + [far] * hbm + [vmem] * (len(args) - scalars - hbm),
        out_specs=[far] * hbm_outs + [vmem] * (len(outs) - hbm_outs),
        out_shape=outs,
        compiler_params=pltpu.CompilerParams(vmem_limit_bytes=mib << 20),
        **extra,
    )(*args)
    return result[0] if len(outs) == 1 else result


def after(value, *others):
    return lax.optimization_barrier((value, *others))[0]


def shape(*dims, dtype=BF):
    return jax.ShapeDtypeStruct(dims, dtype)


def start_kernel(k_hbm, v_hbm, q_hbm, ctx_hbm, w_hbm, cap_hbm, image_hbm, out_ref, k_ref, v_ref, q_ref, ctx_ref, w_ref, cap_ref, image_ref, sems):
    loads = [
        pltpu.make_async_copy(source, target, sems.at[i])
        for i, (source, target) in enumerate(
            ((k_hbm, k_ref), (v_hbm, v_ref), (q_hbm, q_ref), (ctx_hbm, ctx_ref), (w_hbm, w_ref), (cap_hbm, cap_ref))
        )
    ]
    for load in loads:
        load.start()
    for load in loads[:3]:
        load.wait()
    moves = []
    for m in range(GROUP):
        side, head, keys, piece = duty(m)
        cols = slice(head * HD, (head + 1) * HD)
        rows = slice(keys * KEYS, (keys + 1) * KEYS)
        image_ref[m, :KEYS] = k_ref[side, rows, cols]
        image_ref[m, KEYS : 2 * KEYS] = v_ref[side, rows, cols]
        image_ref[m, 2 * KEYS :] = q_ref[side, piece * PIECE : (piece + 1) * PIECE, cols]
        moves.append(pltpu.make_async_copy(image_ref.at[m], image_hbm.at[m], sems.at[len(loads) + m]))
        moves[-1].start()
    for load in loads[3:]:
        load.wait()
    term = lax.dot_general(w_ref[...], ctx_ref[...], NT, preferred_element_type=F32)
    rows = term.shape[1]
    out_ref[:, :rows] = term.astype(BF)
    out_ref[:, rows:] = cap_ref[...]
    for move in moves:
        move.wait()


def near_kernel(own_ref, far_ref, out_ref):
    cols = (out_ref.shape[1] - own_ref.shape[1])
    rows = own_ref.shape[1] - cols
    out_ref[:, :rows] = (own_ref[:, :rows].astype(F32) + far_ref[:, :rows].astype(F32)).astype(BF)
    out_ref[:, rows:] = jnp.concatenate([own_ref[:, rows:], far_ref[:, rows:]], axis=1)


def joint_kernel(pos_ref, n0, n1, n2, n3, res_ref, w_ref, o0, o1, o2, o3, hid_ref):
    x, yhi, zhi = pos_ref[0], pos_ref[1], pos_ref[2]
    rows = hid_ref.shape[1]
    cols = w_ref.shape[0] // (2 * X)
    total = res_ref[...].astype(F32)
    joint = jnp.zeros((total.shape[0], w_ref.shape[1]), F32)
    for step, ref in enumerate((n0, n1, n2, n3)):
        total = total + ref[:, :rows].astype(F32)
        source = (x + X - step) % X
        for far in range(2):
            block = source * 2 + (yhi + far) % 2
            first = pl.multiple_of(block * cols, cols)
            cap = ref[:, rows + far * cols : rows + (far + 1) * cols]
            joint += jnp.dot(cap, w_ref[pl.ds(first, cols), :], preferred_element_type=F32)
    hid_ref[...] = total.astype(BF)
    joint = joint.astype(BF)
    for step, ref in enumerate((o0, o1, o2, o3)):
        first = pl.multiple_of((zhi + step) % Z_HI * TXT, TXT)
        ref[:, :TXT] = hid_ref[:, pl.ds(first, TXT)]
        ref[:, TXT:] = joint


def part_kernel(g0, g1, g2, g3, out_ref):
    part = None
    for ref in (g0, g1, g2, g3):
        term = lax.dot_general(ref[:, :TXT], ref[:, TXT:], TN, preferred_element_type=F32)
        part = term if part is None else part + term
    out_ref[...] = part.astype(BF).reshape(out_ref.shape)


def sum_kernel(part_ref, o_ref, out_ref):
    total = jnp.sum(part_ref[...].astype(F32), axis=0)
    text = jnp.concatenate([total[:, i * HD : (i + 1) * HD] for i in range(4)], axis=0).astype(BF)
    for m in range(GROUP):
        out_ref[m, :TEXT] = o_ref[m]
        out_ref[m, TEXT:] = text


BLOCK = 512


def image_kernel(own_ref, other_ref, out_ref):
    scale = SCALE * LOG2E
    count = BLOCK // PIECE
    for block in range(GROUP // count):
        members = slice(block * count, (block + 1) * count)
        q = own_ref[members, 2 * KEYS :].reshape(BLOCK, HD)
        top, total, acc = jnp.full((BLOCK, 1), NEG, F32), 0.0, 0.0
        for ref in (own_ref, other_ref):
            s = lax.dot_general(q, ref[:, :KEYS].reshape(-1, HD), NT, preferred_element_type=F32)
            old, top = top, jnp.maximum(top, jnp.max(s, axis=1, keepdims=True))
            p = jnp.exp2(s * scale - top * scale)
            factor = jnp.exp2(old * scale - top * scale)
            values = ref[:, KEYS : 2 * KEYS].reshape(-1, HD)
            total = total * factor + jnp.sum(p, axis=1, keepdims=True)
            acc = acc * factor + jnp.dot(p.astype(BF), values, preferred_element_type=F32)
        out_ref[members, :PIECE] = (acc / total).astype(BF).reshape(count, PIECE, HD)
        rest = top * SCALE + jnp.log(total)
        rest = jnp.transpose(jnp.broadcast_to(rest, (BLOCK, HD)))[:8]
        first = rest.astype(BF).astype(F32)
        rest = rest - first
        second = rest.astype(BF).astype(F32)
        place = lax.broadcasted_iota(jnp.int32, rest.shape, 0)
        lse = jnp.where(place == 0, first, jnp.where(place == 1, second, rest - second))
        for i in range(count):
            row = jnp.concatenate([lse[:, i * PIECE : (i + 1) * PIECE]] * 2, axis=1)
            out_ref[block * count + i, LSE:TEXT] = row.astype(BF)


def text_kernel(pair_ref, live_ref, q_ref, back_ref, out_hbm, out_ref, sems):
    live = live_ref[pair_ref[0]]
    text = [
        back_ref[:, TEXT + 8 * i : TEXT + 8 * i + 8].astype(F32).reshape(TXT, HD).astype(BF) for i in range(4)
    ]
    rows = q_ref.shape[1]
    kept = lax.broadcasted_iota(jnp.int32, (rows, TXT), 1) < live
    low = lax.broadcasted_iota(jnp.int32, (1, HD), 1) < PIECE
    units = [(side, head) for side in range(2) for head in range(2)]
    owners = [sorted((m for m in range(GROUP) if duty(m)[:2] == u), key=lambda m: duty(m)[3]) for u in units]
    lse_rows, scores = [], []
    for (side, head), group in zip(units, owners, strict=True):
        tails = [back_ref[m, LSE:TEXT].astype(F32) for m in group]
        lse = [tail[:1] + tail[1:2] + tail[2:3] for tail in tails]
        lse_rows.append(jnp.concatenate([jnp.where(low, lse[0], lse[1]), jnp.where(low, lse[2], lse[3])], axis=1))
        q = q_ref[side, :, head * HD : (head + 1) * HD]
        scores.append(lax.dot_general(q, text[head], NT, preferred_element_type=F32) * SCALE)
    columns = jnp.transpose(jnp.concatenate(lse_rows * 2, axis=0))
    stores = []
    for i, ((side, head), group) in enumerate(zip(units, owners, strict=True)):
        s = jnp.where(kept, scores[i], NEG)
        lse = columns[:, i : i + 1]
        top = jnp.maximum(jnp.max(s, axis=1, keepdims=True), lse)
        p = jnp.exp(s - top)
        image = jnp.exp(lse - top)
        total = image + jnp.sum(p, axis=1, keepdims=True)
        acc = jnp.dot(p.astype(BF), text[2 + head], preferred_element_type=F32)
        acc += image * jnp.concatenate([back_ref[m, :PIECE] for m in group], axis=0).astype(F32)
        out_ref[side, :, head * HD : (head + 1) * HD] = (acc / total).astype(BF)
        if head:
            stores.append(pltpu.make_async_copy(out_ref.at[side], out_hbm.at[side], sems.at[side]))
            stores[-1].start()
    for store in stores:
        store.wait()


def local(
    llama_context,
    llama_residual,
    w_attn_out,
    w_caption,
    w_text_kv,
    prompt_length,
    image_query,
    image_key,
    image_value,
):
    tp, seq = lax.axis_index("tp"), lax.axis_index("seq")
    pos = jnp.stack((tp >> 1, tp & 1, seq >> 4))
    feats, text_rows = w_attn_out.shape[1], llama_context.shape[0]
    w_kv = w_text_kv.reshape(w_text_kv.shape[0], -1)
    kv_cols = w_kv.shape[1]

    cap_cols = w_caption.shape[1]
    image, term = call(
        start_kernel,
        (image_key, image_value, image_query, llama_context, w_attn_out.T, w_caption),
        [shape(GROUP, SENT, HD), shape(feats, text_rows + cap_cols)],
        mib=60,
        hbm=6,
        hbm_outs=1,
        scratch_shapes=[
            *[pltpu.VMEM(image_query.shape, BF)] * 3,
            pltpu.VMEM(llama_context.shape, BF),
            pltpu.VMEM(w_attn_out.shape[::-1], BF),
            pltpu.VMEM(w_caption.shape, BF),
            pltpu.VMEM((GROUP, SENT, HD), BF),
            pltpu.SemaphoreType.DMA((6 + GROUP,)),
        ],
    )
    far = lax.ppermute(term, "tp", [(t, t ^ 1) for t in range(2 * X)])
    own = spread(image)

    near = call(near_kernel, (term, far), [shape(feats, text_rows + 2 * cap_cols)])
    ring = [near]
    for step in range(1, X):
        ring.append(shifted(near, "tp", X, 2, step))
    sends = call(
        joint_kernel,
        (pos, *ring, llama_residual.T, w_kv),
        [shape(feats, TXT + kv_cols)] * Z_HI,
        scalars=1,
        mib=8,
        scratch_shapes=[pltpu.VMEM((feats, text_rows), BF)],
    )
    parts = [sends[0]]
    for step in range(1, Z_HI):
        parts.append(shifted(sends[step], "seq", Z_HI, GROUP, step))
    own = after(own, sends[0])
    other = lax.ppermute(own, "seq", [(i, i ^ 1) for i in range(Z_HI * GROUP)])
    part = call(part_kernel, parts, [shape(GROUP, TXT // GROUP, kv_cols)])
    part = spread(part)
    o = call(image_kernel, (own, other), [shape(GROUP, TEXT, HD)], mib=32)
    back = call(sum_kernel, (after(part, o), o), [shape(GROUP, BACK, HD)])
    back = spread(back)
    return call(
        text_kernel,
        (pos[2:], prompt_length, image_query, back),
        [shape(*image_query.shape)],
        scalars=2,
        hbm_outs=1,
        scratch_shapes=[pltpu.VMEM(image_query.shape, BF), pltpu.SemaphoreType.DMA((image_query.shape[0],))],
    )


def solution(mesh):
    placed = (
        P(None, "tp"),
        P(None, "seq"),
        P("tp", "seq"),
        P("seq", "tp"),
        P(None, None, "tp"),
        P(),
        P(None, "seq", "tp"),
        P(None, "seq", "tp"),
        P(None, "seq", "tp"),
    )

    return jax.shard_map(local, mesh=mesh, in_specs=placed, out_specs=P(None, "seq", "tp"), check_vma=False)
```
